32 devices in a mesh: row: 2 (over x), col: 16 (over z, y, core).
Axes of the slice: x: 2, y: 2, z: 4, core: 2. Of those that a mesh axis runs over, the one named last changes fastest.
Arguments:
- features: bfloat16 [8192, 256], P(('row', 'col')), may hold values from -6 to 6
- weight: bfloat16 [256, 128], replicated, may hold values from -0.375 to 0.375
- tiles: bfloat16 [2, 16, 320, 128, 128], P('row', 'col'), may hold values from -0.0625 to 0.0625
- slot_tile_row: int32 [2, 16, 320], P('row', 'col'), may hold values from 0 to 3
- tile_cols: int32 [2, 16, 320], P('row', 'col'), may hold values from 0 to 31
- live_tiles: int32 [2, 16], P('row', 'col'), may hold values from 40 to 320, as said below
- cotangent: bfloat16 [8192, 128], P(('row', 'col')), may hold values from -6 to 6
Outputs:
- logits: bfloat16 [8192, 128], P(('row', 'col'))
- grad_features: bfloat16 [8192, 256], P(('row', 'col'))
- grad_weight: float32 [256, 128], replicated
The draws below stay inside these ranges and needn't reach their ends.
Inputs may be any that keep to these rules, and one draw needn't show every extreme that they name: Slots of a block from live_tiles on are padding and not part of the adjacency; in every draw some block has all 320 slots live.
All inputs are finite; a program needn't handle non-finite values.
Results may differ from the reference program's by a relative error of at most 0.005.
Values may be sent and summed in bfloat16 or wider, within the bound.
A program may use at most 128 MiB of HBM per device.

```python
import math
import jax
import jax.numpy as jnp
from jax import lax

F = 256
FO = 128
TILE = 128
CH = 256
NT = 320
NODES = 8192
ROW_TILES = 4
COL_TILES = 32
N_ROW = 2
N_COL = 16


def draw_live_tiles(key, part):
    key_base, key_heavy, key_forced = jax.random.split(key, 3)
    grid_shape = (N_ROW, N_COL)
    base_count = jax.random.randint(key_base, grid_shape, NT // 8, NT // 2 + 1)
    heavy_rows = jax.random.randint(key_heavy, grid_shape, 0, 4) == 0
    counts = jnp.where(heavy_rows, NT, base_count).reshape(-1)
    forced_index = jax.random.randint(key_forced, (), 0, N_ROW * N_COL)
    counts = jnp.where(jnp.arange(N_ROW * N_COL) == forced_index, NT, counts)
    return counts.reshape(grid_shape).astype(jnp.int32)


def touch_ends(result, rng, smallest, high):
    extent = result.shape
    place = [jax.random.randint(jax.random.fold_in(rng, axis), (), 0, extent[axis]) for axis in range(len(extent))]
    result = result.at[tuple(place)].set(smallest)
    longest = extent.index(max(extent))
    place[longest] = (place[longest] + 1) % extent[longest]
    return result.at[tuple(place)].set(high)


def level_of(own_key, shape, shards, smallest, high):
    gain = 1.0
    for axis_at, shards_of in shards:
        steps = jax.random.uniform(jax.random.fold_in(jax.random.fold_in(own_key, 6), axis_at), (shards_of,), jnp.float32, smallest / len(shards), high / len(shards))
        gain = gain * jnp.repeat(jnp.exp(steps), shape[axis_at] // shards_of).reshape((-1,) + (1,) * (len(shape) - 1 - axis_at))
    return gain


def gaussian(stream_key, extent, spread, most, cuts=(), kind=jnp.bfloat16):
    entries = spread * jax.random.normal(stream_key, extent, jnp.float32)
    if cuts:
        entries = entries * level_of(stream_key, extent, cuts, -0.22, 0.18)
    return jnp.clip(entries, -most, most).astype(kind)


def setup_inputs(seed: int = 0) -> dict:
    keys = jax.random.split(jax.random.key(seed), 8)
    return {
        "features": gaussian(keys[0], (NODES, F), 1.0, 6.0, ((0, 32),)),
        "weight": gaussian(keys[1], (F, FO), F ** -0.5, 0.375),
        "tiles": gaussian(keys[2], (N_ROW, N_COL, NT, TILE, TILE), (NT * TILE * TILE // (2 * CH)) ** -0.5, 0.0625, ((0, 2), (1, 16))),
        "slot_tile_row": touch_ends(jax.random.randint(keys[3], (N_ROW, N_COL, NT), 0, ROW_TILES), jax.random.fold_in(keys[3], 1), 0, ROW_TILES - 1).astype(jnp.int32),
        "tile_cols": touch_ends(jax.random.randint(keys[4], (N_ROW, N_COL, NT), 0, COL_TILES), jax.random.fold_in(keys[4], 1), 0, COL_TILES - 1).astype(jnp.int32),
        "live_tiles": draw_live_tiles(jax.random.fold_in(keys[7], 71), 0),
        "cotangent": gaussian(keys[6], (NODES, FO), 1.0, 6.0, ((0, 32),)),
    }


def device_products(tile_block, row_slots, col_slots, live_count, projected_group, cot_group):
    tiles_wide = tile_block.astype(jnp.float32)
    live_mask = jnp.arange(NT, dtype=jnp.int32) < live_count
    inputs = projected_group.astype(jnp.float32).reshape(COL_TILES, TILE, FO)[col_slots]
    products = jnp.einsum('tab,tbf->taf', tiles_wide, inputs, precision=lax.Precision.HIGHEST)
    row_onehot = ((row_slots[None, :] == jnp.arange(ROW_TILES, dtype=jnp.int32)[:, None]) & live_mask[None, :]).astype(jnp.float32)
    forward = jnp.einsum('rt,taf->raf', row_onehot, products, precision=lax.Precision.HIGHEST)
    cot_tiles = cot_group.astype(jnp.float32).reshape(ROW_TILES, TILE, FO)[row_slots]
    backward_partials = jnp.einsum('tab,taf->tbf', tiles_wide, cot_tiles, precision=lax.Precision.HIGHEST)
    column_indicator = ((col_slots[None, :] == jnp.arange(COL_TILES, dtype=jnp.int32)[:, None]) & live_mask[None, :]).astype(jnp.float32)
    backward_layer_pass = jnp.einsum('io,owe->iwe', column_indicator, backward_partials, precision=lax.Precision.HIGHEST)
    return (forward.reshape(ROW_TILES * TILE, FO), backward_layer_pass.reshape(COL_TILES * TILE, FO))

def reference(features, weight, tiles, slot_tile_row, tile_cols, live_tiles, cotangent):
    projected = jnp.dot(features, weight, preferred_element_type=jnp.float32).astype(jnp.bfloat16)
    proj_groups = projected.reshape(N_ROW, N_COL * CH, FO)
    cot_stretches = cotangent.reshape(N_ROW, N_COL, CH, FO)
    device_total = N_ROW * N_COL

    def visit(carry, inputs):
        logit_sums, back_sums = carry
        position, tile_block, row_slots, col_slots, live_count = inputs
        group_index = position // N_COL
        column_index = position % N_COL
        projected_group = proj_groups[group_index]
        cot_group = cot_stretches[:, column_index].reshape(N_ROW * CH, FO)
        forward, backward_layer_pass = device_products(tile_block, row_slots, col_slots, live_count, projected_group, cot_group)
        logit_sums = logit_sums.at[:, column_index].add(forward.reshape(N_ROW, CH, FO))
        back_sums = back_sums.at[group_index].add(backward_layer_pass)
        return ((logit_sums, back_sums), None)
    start_sums = (jnp.zeros((N_ROW, N_COL, CH, FO), jnp.float32), jnp.zeros((N_ROW, N_COL * CH, FO), jnp.float32))
    scanned = (jnp.arange(device_total, dtype=jnp.int32), tiles.reshape(device_total, NT, TILE, TILE), slot_tile_row.reshape(device_total, NT), tile_cols.reshape(device_total, NT), live_tiles.reshape(device_total))
    (logit_sums, back_sums), unused = lax.scan(visit, start_sums, scanned)
    logits = logit_sums.reshape(NODES, FO).astype(jnp.bfloat16)
    back_rounded = back_sums.reshape(NODES, FO).astype(jnp.bfloat16)
    grad_features = jnp.dot(back_rounded, weight.T, preferred_element_type=jnp.float32).astype(jnp.bfloat16)
    grad_weight = jnp.dot(features.T, back_rounded, preferred_element_type=jnp.float32) / math.sqrt(NODES)
    return (logits, grad_features, grad_weight)
```

```python
import functools
import math

import jax
import jax.numpy as jnp
from jax import lax
from jax.experimental import pallas as pl
from jax.experimental.pallas import tpu as pltpu
from jax.sharding import PartitionSpec as P

MESH = pl.DeviceIdType.MESH
F32 = jnp.float32
BF16 = jnp.bfloat16


def kernel(dims, features, weight, tiles, slot_rows, slot_cols, live, cot,
           logits, grad_features, grad_weight,
           tile_buf, sums, proj, cots, cots_t, feat_t, code_v, last_v, code, last,
           sib_out, sib_in, y_out, y_in, z_out, z_in, log_out, log_in,
           term_out, term_in, total,
           tile_sem, smem_sem, cot_send, cot_recv, ag_send, ag_recv,
           sib_send, sib_recv, y_send, y_recv, z_send, z_recv,
           log_send, log_recv, term_send, term_recv, tot_send, tot_recv):
    R, C, O, I = dims
    n = R * C
    slots = tiles.shape[0]
    side = tiles.shape[1]
    stretch = features.shape[0]
    per = stretch // side
    col_tiles = C * per
    cells = R * per * col_tiles
    r, c = lax.axis_index("row"), lax.axis_index("col")
    me = r * C + c
    k = lax.rem(c, 2)
    q = c // 2
    y = lax.rem(q, I)
    z = q // I

    def col_of(zz, yy, kk):
        return (zz * I + yy) * 2 + kk

    def remote(src, dst, send, recv, dev):
        return pltpu.make_async_remote_copy(
            src_ref=src, dst_ref=dst, send_sem=send, recv_sem=recv,
            device_id=dev, device_id_type=MESH)

    chunks = tile_sem.shape[0]
    chunk = slots // chunks
    loads = [
        pltpu.make_async_copy(tiles.at[pl.ds(i * chunk, chunk)],
                              tile_buf.at[pl.ds(i * chunk, chunk)], tile_sem.at[i])
        for i in range(chunks)
    ]
    for load in loads:
        load.start()

    barrier = pltpu.get_barrier_semaphore()

    def greet(d, carry):
        t = lax.rem(me + d, n)
        pl.semaphore_signal(barrier, inc=1, device_id=(t // C, lax.rem(t, C)), device_id_type=MESH)
        return carry

    lax.fori_loop(1, n, greet, 0)
    proj[c] = jnp.dot(features[...], weight[...], preferred_element_type=F32).astype(BF16)
    pl.semaphore_wait(barrier, n - 1)

    pending = []

    def gather_send(block, dev):
        copy = remote(proj.at[block], proj.at[block], ag_send.at[len(pending)],
                      ag_recv.at[block], (r, dev))
        copy.start()
        pending.append(copy)

    def gather_wait(block):
        remote(proj.at[block], proj.at[block], ag_send.at[0], ag_recv.at[block],
               (r, c)).wait_recv()

    cot_copies = []
    for d in range(1, R):
        peer = lax.rem(r + d, R)
        copy = remote(cot, cots.at[r], cot_send.at[d], cot_recv.at[r], (peer, c))
        copy.start()
        cot_copies.append(copy)
    z_peers = [lax.rem(z + d, O) for d in range(1, O)]
    y_peers = [lax.rem(y + d, I) for d in range(1, I)]
    for yy in y_peers:
        gather_send(c, col_of(z, yy, k))
    for zz in z_peers:
        gather_send(c, col_of(zz, y, k))
    gather_send(c, col_of(z, y, 1 - k))

    lane = lax.broadcasted_iota(jnp.int32, (1, slots), 1)
    cell = jnp.where(lane < live[0, 0], slot_rows[...] * col_tiles + slot_cols[...], cells)
    eye = (lax.broadcasted_iota(jnp.int32, (slots, slots), 0)
           == lax.broadcasted_iota(jnp.int32, (slots, slots), 1))
    cell_c = jnp.sum(jnp.where(eye, cell, 0), axis=1, keepdims=True)
    sub = lax.broadcasted_iota(jnp.int32, (slots, 1), 0)
    same_before = (cell == cell_c) & (lane < sub)
    rank = jnp.sum(((cell < cell_c) | same_before).astype(jnp.int32), axis=1, keepdims=True)
    keep = jnp.max(same_before.astype(jnp.int32), axis=1, keepdims=True)
    code_v[...] = jnp.sum(jnp.where(rank == lane, sub * 2 + keep, 0), axis=0, keepdims=True)
    cell_ids = lax.broadcasted_iota(jnp.int32, (1, cells), 1)
    upto = jnp.sum((cell_c <= cell_ids).astype(jnp.int32), axis=0, keepdims=True)
    held = jnp.max((cell_c == cell_ids).astype(jnp.int32), axis=0, keepdims=True)
    last_v[...] = upto * held
    to_smem = [pltpu.make_async_copy(code_v, code, smem_sem.at[0]),
               pltpu.make_async_copy(last_v, last, smem_sem.at[1])]
    for copy in to_smem:
        copy.start()
    feat_t[...] = features[...].astype(F32).T.astype(BF16)
    cots_t[r] = cot[...].astype(F32).T.astype(BF16)
    sums[0] = jnp.zeros((side, side), BF16)
    for copy in to_smem:
        copy.wait()
    for load in loads:
        load.wait()

    def add_slot(j, acc):
        word = code[0, j]
        keep_it = lax.rem(word, 2).astype(F32)
        acc = acc * keep_it + tile_buf[word // 2].astype(F32)
        sums[j + 1] = acc.astype(BF16)
        return acc

    parts = 4
    acc = jnp.zeros((side, side), F32)
    for part in range(parts):
        acc = lax.fori_loop(part * slots // parts, (part + 1) * slots // parts, add_slot, acc,
                            unroll=2)
        if part == 1:
            for zz in z_peers:
                block = col_of(zz, y, k)
                gather_wait(block)
                for yy in y_peers:
                    gather_send(block, col_of(z, yy, k))
                gather_send(block, col_of(z, y, 1 - k))
        if part == parts - 1:
            for d in range(O):
                zz = lax.rem(z + d, O)
                for yy in y_peers:
                    block = col_of(zz, yy, k)
                    gather_wait(block)
                    gather_send(block, col_of(z, y, 1 - k))

    for d in range(1, R):
        peer = lax.rem(r + d, R)
        remote(cot, cots.at[peer], cot_send.at[d], cot_recv.at[peer], (peer, c)).wait_recv()
        cots_t[peer] = cots[peer].astype(F32).T.astype(BF16)

    def stretch_block(s, b):
        rows = []
        for a in range(per):
            base = (s * per + a) * col_tiles + b * per
            rows.append(jnp.concatenate([sums[last[0, base + e]] for e in range(per)], axis=1))
        return jnp.concatenate(rows, axis=0)

    def back_block(b):
        out = jnp.dot(cots_t[0], stretch_block(0, b), preferred_element_type=F32)
        for s in range(1, R):
            out = out + jnp.dot(cots_t[s], stretch_block(s, b), preferred_element_type=F32)
        return out

    def place(i):
        zz = lax.rem(z + lax.rem(i, O) + 1, O)
        yy = lax.rem(y + i // O + 1, I)
        return zz, yy

    def sib_copy(m):
        return remote(sib_out.at[m], sib_in.at[m], sib_send.at[m], sib_recv.at[m],
                      (r, col_of(z, y, 1 - k)))

    def send_sib(i, carry):
        zz, yy = place(i)
        m = zz * I + yy
        sib_out[m] = back_block(2 * m + 1 - k).astype(BF16)
        sib_copy(m).start()
        return carry

    lax.fori_loop(0, O * I, send_sib, 0)

    def y_copy(zz, yy):
        return remote(y_out.at[zz * I + yy], y_in.at[y * O + zz], y_send.at[zz * I + yy],
                      y_recv.at[y * O + zz], (r, col_of(z, yy, k)))

    def send_y(i, carry):
        zz, yy = place(i)
        m = zz * I + yy
        mine = back_block(2 * m + k)
        sib_copy(m).wait_recv()
        y_out[m] = (mine + sib_in[m].astype(F32)).astype(BF16)
        y_copy(zz, yy).start()
        return carry

    lax.fori_loop(0, O * (I - 1), send_y, 0)

    for d in range(O):
        for e in range(I):
            gather_wait(col_of(lax.rem(z + d, O), lax.rem(y + e, I), 1 - k))
    group = 4 if C % 4 == 0 else 1

    def forward(s):
        def step(g, out):
            for b in range(group):
                out = out + jnp.dot(stretch_block(s, g * group + b), proj[g * group + b],
                                    preferred_element_type=F32)
            return out
        return lax.fori_loop(0, C // group, step, jnp.zeros((stretch, proj.shape[2]), F32))

    log_copies = []
    for d in range(1, R):
        peer = lax.rem(r + d, R)
        log_out[d - 1] = forward(peer)
        copy = remote(log_out.at[d - 1], log_in.at[r], log_send.at[d], log_recv.at[r], (peer, c))
        copy.start()
        log_copies.append(copy)
    mine_log = forward(r)

    def summed(zz):
        m = zz * I + y
        value = back_block(2 * m + k)
        sib_copy(m).wait_recv()
        value = value + sib_in[m].astype(F32)
        for yy in y_peers:
            slot = yy * O + zz
            remote(y_out.at[0], y_in.at[slot], y_send.at[0], y_recv.at[slot],
                   (r, c)).wait_recv()
            value = value + y_in[slot].astype(F32)
        return value

    z_copies = []
    for d in range(1, O):
        zz = lax.rem(z + d, O)
        z_out[d - 1] = summed(zz).astype(BF16)
        copy = remote(z_out.at[d - 1], z_in.at[z], z_send.at[d - 1], z_recv.at[z],
                      (r, col_of(zz, y, k)))
        copy.start()
        z_copies.append(copy)
    back_t = summed(z)
    for d in range(1, R):
        peer = lax.rem(r + d, R)
        remote(log_out.at[0], log_in.at[peer], log_send.at[0], log_recv.at[peer],
               (peer, c)).wait_recv()
        mine_log = mine_log + log_in[peer]
    logits[...] = mine_log.astype(BF16)
    for zz in z_peers:
        remote(z_out.at[0], z_in.at[zz], z_send.at[0], z_recv.at[zz], (r, c)).wait_recv()
        back_t = back_t + z_in[zz].astype(F32)
    back = back_t.T.astype(BF16)
    term = jnp.dot(feat_t[...], back, preferred_element_type=F32)

    owners = term_out.shape[0]
    rows = term_out.shape[1]
    term_out[...] = term.reshape(term_out.shape)

    def term_copy(t):
        return remote(term_out.at[t], term_in.at[me], term_send.at[t], term_recv.at[me],
                      (t // C, lax.rem(t, C)))

    def term_arrival(t):
        return remote(term_out.at[0], term_in.at[t], term_send.at[0], term_recv.at[t], (r, c))

    def tot_copy(t):
        return remote(total.at[me], total.at[me], tot_send.at[t], tot_recv.at[me],
                      (t // C, lax.rem(t, C)))

    def tot_arrival(t):
        return remote(total.at[t], total.at[t], tot_send.at[0], tot_recv.at[t], (r, c))

    def others(count, act):
        def body(d, carry):
            t = lax.rem(me + d, n)
            if count == n:
                act(t)
            else:
                @pl.when(t < count)
                def _():
                    act(t)
            return carry
        lax.fori_loop(1, n, body, 0)

    def own_part():
        term_in[me] = term_out[me]
        others(n, lambda t: term_arrival(t).wait_recv())
        total[me] = jnp.sum(term_in[...], axis=0) * (1.0 / math.sqrt(n * stretch))
        others(n, lambda t: tot_copy(t).start())

    others(owners, lambda t: term_copy(t).start())
    grad_features[...] = lax.dot_general(
        back, weight[...], (((1,), (1,)), ((), ())), preferred_element_type=F32).astype(BF16)
    if owners == n:
        own_part()
    else:
        pl.when(me < owners)(own_part)
    for copy in pending + cot_copies + log_copies + z_copies:
        copy.wait_send()

    def drain_sib(m, carry):
        sib_copy(m).wait_send()
        return carry

    lax.fori_loop(0, O * I, drain_sib, 0)

    def drain_y(i, carry):
        zz, yy = place(i)
        y_copy(zz, yy).wait_send()
        return carry

    lax.fori_loop(0, O * (I - 1), drain_y, 0)
    others(owners, lambda t: term_copy(t).wait_send())
    others(owners, lambda t: tot_arrival(t).wait_recv())
    grad_weight[...] = total[...].reshape(grad_weight.shape)
    if owners == n:
        others(n, lambda t: tot_copy(t).wait_send())
    else:
        @pl.when(me < owners)
        def _():
            others(n, lambda t: tot_copy(t).wait_send())


def per_device(R, C, features, weight, tiles, slot_tile_row, tile_cols, live_tiles, cotangent):
    slots, side = tiles.shape[2], tiles.shape[3]
    stretch, width = features.shape
    out_width = weight.shape[1]
    half = C // 2
    O = 4 if half % 4 == 0 else half
    I = half // O
    n = R * C
    per = stretch // side
    cells = R * per * C * per
    owners = min(n, width // 8)
    rows = width // owners
    chunks = 8 if slots % 8 == 0 else 1
    dma = pltpu.SemaphoreType.DMA
    vmem = pltpu.VMEM
    blk = (out_width, stretch)
    gathers = (O - 1) + (I - 1) + 1 + (O - 1) * I + O * (I - 1)
    scratch = [
        vmem((slots, side, side), BF16),
        vmem((slots + 1, side, side), BF16),
        vmem((C, stretch, out_width), BF16),
        vmem((R, stretch, out_width), BF16),
        vmem((R,) + blk, BF16),
        vmem((width, stretch), BF16),
        vmem((1, slots), jnp.int32),
        vmem((1, cells), jnp.int32),
        pltpu.SMEM((1, slots), jnp.int32),
        pltpu.SMEM((1, cells), jnp.int32),
        vmem((half,) + blk, BF16),
        vmem((half,) + blk, BF16),
        vmem((half,) + blk, BF16),
        vmem((half,) + blk, BF16),
        vmem((max(O - 1, 1),) + blk, BF16),
        vmem((O,) + blk, BF16),
        vmem((max(R - 1, 1), stretch, out_width), F32),
        vmem((R, stretch, out_width), F32),
        vmem((owners, rows, out_width), F32),
        vmem((n, rows, out_width), F32),
        vmem((owners, rows, out_width), F32),
        dma((chunks,)), dma((2,)), dma((R,)), dma((R,)),
        dma((gathers,)), dma((C,)),
        dma((half,)), dma((half,)), dma((half,)), dma((half,)),
        dma((O,)), dma((O,)), dma((R,)), dma((R,)),
        dma((n,)), dma((n,)), dma((n,)), dma((n,)),
    ]
    v = pl.BlockSpec(memory_space=pltpu.VMEM)
    return pl.pallas_call(
        functools.partial(kernel, (R, C, O, I)),
        out_shape=(
            jax.ShapeDtypeStruct((stretch, out_width), BF16),
            jax.ShapeDtypeStruct((stretch, width), BF16),
            jax.ShapeDtypeStruct((width, out_width), F32),
        ),
        in_specs=[v, v, pl.BlockSpec(memory_space=pl.ANY), v, v,
                  pl.BlockSpec(memory_space=pltpu.SMEM), v],
        out_specs=(v, v, v),
        scratch_shapes=scratch,
        compiler_params=pltpu.CompilerParams(
            collective_id=0, has_side_effects=True, vmem_limit_bytes=60 * 1024 * 1024),
    )(features, weight, tiles.reshape(slots, side, side), slot_tile_row.reshape(1, slots),
      tile_cols.reshape(1, slots), live_tiles, cotangent)


def solution(mesh):
    R, C = mesh.shape["row"], mesh.shape["col"]
    placed = (
        P(("row", "col"), None),
        P(),
        P("row", "col", None, None, None),
        P("row", "col", None),
        P("row", "col", None),
        P("row", "col"),
        P(("row", "col"), None),
    )
    return jax.shard_map(
        functools.partial(per_device, R, C),
        mesh=mesh,
        in_specs=placed,
        out_specs=(P(("row", "col"), None), P(("row", "col"), None), P()),
        check_vma=False,
    )
```

```python
import functools
import math

import jax
import jax.numpy as jnp
from jax import lax
from jax.experimental import pallas as pl
from jax.experimental.pallas import tpu as pltpu
from jax.sharding import PartitionSpec as P

MESH = pl.DeviceIdType.MESH
F32 = jnp.float32
BF16 = jnp.bfloat16


def kernel(dims, features, weight, tiles, slot_rows, slot_cols, live, cot,
           logits, grad_features, grad_weight,
           tile_buf, sums, proj, cots, cots_t, feat_t, code_v, last_v, code, last,
           sib_out, sib_in, y_out, y_in, z_out, z_in, log_out, log_in,
           term_out, term_in, total,
           tile_sem, smem_sem, cot_send, cot_recv, ag_send, ag_recv,
           sib_send, sib_recv, y_send, y_recv, z_send, z_recv,
           log_send, log_recv, term_send, term_recv, tot_send, tot_recv):
    R, C, O, I = dims
    n = R * C
    slots = tiles.shape[0]
    side = tiles.shape[1]
    stretch = features.shape[0]
    per = stretch // side
    col_tiles = C * per
    cells = R * per * col_tiles
    r, c = lax.axis_index("row"), lax.axis_index("col")
    me = r * C + c
    k = lax.rem(c, 2)
    q = c // 2
    y = lax.rem(q, I)
    z = q // I

    def col_of(zz, yy, kk):
        return (zz * I + yy) * 2 + kk

    def remote(src, dst, send, recv, dev):
        return pltpu.make_async_remote_copy(
            src_ref=src, dst_ref=dst, send_sem=send, recv_sem=recv,
            device_id=dev, device_id_type=MESH)

    chunks = tile_sem.shape[0]
    chunk = slots // chunks
    loads = [
        pltpu.make_async_copy(tiles.at[pl.ds(i * chunk, chunk)],
                              tile_buf.at[pl.ds(i * chunk, chunk)], tile_sem.at[i])
        for i in range(chunks)
    ]
    for load in loads:
        load.start()

    barrier = pltpu.get_barrier_semaphore()

    def greet(d, carry):
        t = lax.rem(me + d, n)
        pl.semaphore_signal(barrier, inc=1, device_id=(t // C, lax.rem(t, C)), device_id_type=MESH)
        return carry

    lax.fori_loop(1, n, greet, 0, unroll=n - 1 if n <= 32 else 1)
    proj[c] = jnp.dot(features[...], weight[...], preferred_element_type=F32).astype(BF16)
    lane = lax.broadcasted_iota(jnp.int32, (1, slots), 1)
    cell = jnp.where(lane < live[0, 0], slot_rows[...] * col_tiles + slot_cols[...], cells)
    eye = (lax.broadcasted_iota(jnp.int32, (slots, slots), 0)
           == lax.broadcasted_iota(jnp.int32, (slots, slots), 1))
    cell_c = jnp.sum(jnp.where(eye, cell, 0), axis=1, keepdims=True)
    sub = lax.broadcasted_iota(jnp.int32, (slots, 1), 0)
    same_before = (cell == cell_c) & (lane < sub)
    rank = jnp.sum(((cell < cell_c) | same_before).astype(jnp.int32), axis=1, keepdims=True)
    keep = jnp.max(same_before.astype(jnp.int32), axis=1, keepdims=True)
    code_v[...] = jnp.sum(jnp.where(rank == lane, sub * 2 + keep, 0), axis=0, keepdims=True)
    cell_ids = lax.broadcasted_iota(jnp.int32, (1, cells), 1)
    upto = jnp.sum((cell_c <= cell_ids).astype(jnp.int32), axis=0, keepdims=True)
    held = jnp.max((cell_c == cell_ids).astype(jnp.int32), axis=0, keepdims=True)
    last_v[...] = upto * held
    to_smem = [pltpu.make_async_copy(code_v, code, smem_sem.at[0]),
               pltpu.make_async_copy(last_v, last, smem_sem.at[1])]
    for copy in to_smem:
        copy.start()
    feat_t[...] = features[...].astype(F32).T.astype(BF16)
    cots_t[r] = cot[...].astype(F32).T.astype(BF16)
    sums[0] = jnp.zeros((side, side), BF16)
    pl.semaphore_wait(barrier, n - 1)

    pending = []

    def gather_send(block, dev):
        copy = remote(proj.at[block], proj.at[block], ag_send.at[len(pending)],
                      ag_recv.at[block], (r, dev))
        copy.start()
        pending.append(copy)

    def gather_wait(block):
        remote(proj.at[block], proj.at[block], ag_send.at[0], ag_recv.at[block],
               (r, c)).wait_recv()

    cot_copies = []
    for d in range(1, R):
        peer = lax.rem(r + d, R)
        copy = remote(cot, cots.at[r], cot_send.at[d], cot_recv.at[r], (peer, c))
        copy.start()
        cot_copies.append(copy)
    z_peers = [lax.rem(z + d, O) for d in range(1, O)]
    y_peers = [lax.rem(y + d, I) for d in range(1, I)]
    for yy in y_peers:
        gather_send(c, col_of(z, yy, k))
    for zz in z_peers:
        gather_send(c, col_of(zz, y, k))
    gather_send(c, col_of(z, y, 1 - k))

    for copy in to_smem:
        copy.wait()
    for load in loads:
        load.wait()

    def add_slot(j, acc):
        word = code[0, j]
        keep_it = lax.rem(word, 2).astype(F32)
        acc = acc * keep_it + tile_buf[word // 2].astype(F32)
        sums[j + 1] = acc.astype(BF16)
        return acc

    parts = 8
    acc = jnp.zeros((side, side), F32)
    for part in range(parts):
        acc = lax.fori_loop(part * slots // parts, (part + 1) * slots // parts, add_slot, acc,
                            unroll=4)
        for zz in z_peers[part - 2:part - 1] if part > 1 else []:
            block = col_of(zz, y, k)
            gather_wait(block)
            for yy in y_peers:
                gather_send(block, col_of(z, yy, k))
            gather_send(block, col_of(z, y, 1 - k))

    for d in range(1, R):
        peer = lax.rem(r + d, R)
        remote(cot, cots.at[peer], cot_send.at[d], cot_recv.at[peer], (peer, c)).wait_recv()
        cots_t[peer] = cots[peer].astype(F32).T.astype(BF16)

    def stretch_block(s, b):
        rows = []
        for a in range(per):
            base = (s * per + a) * col_tiles + b * per
            rows.append(jnp.concatenate([sums[last[0, base + e]] for e in range(per)], axis=1))
        return jnp.concatenate(rows, axis=0)

    def back_block(b):
        out = jnp.dot(cots_t[0], stretch_block(0, b), preferred_element_type=F32)
        for s in range(1, R):
            out = out + jnp.dot(cots_t[s], stretch_block(s, b), preferred_element_type=F32)
        return out

    def place(i):
        zz = lax.rem(z + lax.rem(i, O) + 1, O)
        yy = lax.rem(y + i // O + 1, I)
        return zz, yy

    def sib_copy(m):
        return remote(sib_out.at[m], sib_in.at[m], sib_send.at[m], sib_recv.at[m],
                      (r, col_of(z, y, 1 - k)))

    def send_sib(i, carry):
        zz, yy = place(i)
        m = zz * I + yy
        sib_out[m] = back_block(2 * m + 1 - k).astype(BF16)
        sib_copy(m).start()
        return carry

    lax.fori_loop(0, O * I, send_sib, 0)

    def y_copy(zz, yy):
        return remote(y_out.at[zz * I + yy], y_in.at[y * O + zz], y_send.at[zz * I + yy],
                      y_recv.at[y * O + zz], (r, col_of(z, yy, k)))

    def send_y(i, carry):
        zz, yy = place(i)
        m = zz * I + yy
        mine = back_block(2 * m + k)
        sib_copy(m).wait_recv()
        y_out[m] = (mine + sib_in[m].astype(F32)).astype(BF16)
        y_copy(zz, yy).start()
        return carry

    lax.fori_loop(0, O * (I - 1), send_y, 0)

    for d in range(O):
        zz = lax.rem(z + d, O)
        for yy in y_peers:
            block = col_of(zz, yy, k)
            gather_wait(block)
            gather_send(block, col_of(z, y, 1 - k))

    for d in range(O):
        for e in range(I):
            gather_wait(col_of(lax.rem(z + d, O), lax.rem(y + e, I), 1 - k))
    group = 4 if C % 4 == 0 else 1

    def forward(s):
        def step(g, out):
            for b in range(group):
                out = out + jnp.dot(stretch_block(s, g * group + b), proj[g * group + b],
                                    preferred_element_type=F32)
            return out
        return lax.fori_loop(0, C // group, step, jnp.zeros((stretch, proj.shape[2]), F32))

    log_copies = []
    for d in range(1, R):
        peer = lax.rem(r + d, R)
        log_out[d - 1] = forward(peer)
        copy = remote(log_out.at[d - 1], log_in.at[r], log_send.at[d], log_recv.at[r], (peer, c))
        copy.start()
        log_copies.append(copy)
    mine_log = forward(r)

    def summed(zz):
        m = zz * I + y
        value = back_block(2 * m + k)
        sib_copy(m).wait_recv()
        value = value + sib_in[m].astype(F32)
        for yy in y_peers:
            slot = yy * O + zz
            remote(y_out.at[0], y_in.at[slot], y_send.at[0], y_recv.at[slot],
                   (r, c)).wait_recv()
            value = value + y_in[slot].astype(F32)
        return value

    z_copies = []
    for d in range(1, O):
        zz = lax.rem(z + d, O)
        z_out[d - 1] = summed(zz).astype(BF16)
        copy = remote(z_out.at[d - 1], z_in.at[z], z_send.at[d - 1], z_recv.at[z],
                      (r, col_of(zz, y, k)))
        copy.start()
        z_copies.append(copy)
    back_t = summed(z)
    for d in range(1, R):
        peer = lax.rem(r + d, R)
        remote(log_out.at[0], log_in.at[peer], log_send.at[0], log_recv.at[peer],
               (peer, c)).wait_recv()
        mine_log = mine_log + log_in[peer]
    logits[...] = mine_log.astype(BF16)
    for zz in z_peers:
        remote(z_out.at[0], z_in.at[zz], z_send.at[0], z_recv.at[zz], (r, c)).wait_recv()
        back_t = back_t + z_in[zz].astype(F32)
    back = back_t.T.astype(BF16)
    term = jnp.dot(feat_t[...], back, preferred_element_type=F32)

    owners = term_out.shape[0]
    rows = term_out.shape[1]
    term_out[...] = term.reshape(term_out.shape)

    def term_copy(t):
        return remote(term_out.at[t], term_in.at[me], term_send.at[0], term_recv.at[0],
                      (t // C, lax.rem(t, C)))

    def bulk(count, send, recv):
        part = term_in.at[pl.ds(0, count)]
        return remote(part, part, send.at[0], recv.at[0], (r, c))

    def arrived(count, send, recv):
        bulk(count, send, recv).wait_recv()

    def sent(count, send, recv):
        bulk(count, send, recv).wait_send()

    def by_role(act, send, recv):
        if owners == n:
            act(n - 1, send, recv)
        else:
            pl.when(me < owners)(lambda: act(owners - 1, send, recv))
            pl.when(me >= owners)(lambda: act(owners, send, recv))

    def tot_copy(t):
        return remote(total.at[me], total.at[me], tot_send.at[0], tot_recv.at[0],
                      (t // C, lax.rem(t, C)))

    def others(count, act):
        def body(d, carry):
            t = lax.rem(me + d, n)
            if count == n:
                act(t)
            else:
                @pl.when(t < count)
                def _():
                    act(t)
            return carry
        lax.fori_loop(1, n, body, 0, unroll=n - 1 if n <= 32 else 1)

    def own_part():
        term_in[me] = term_out[me]
        arrived(n - 1, term_send, term_recv)
        total[me] = jnp.sum(term_in[...], axis=0) * (1.0 / math.sqrt(n * stretch))
        others(n, lambda t: tot_copy(t).start())

    others(owners, lambda t: term_copy(t).start())
    grad_features[...] = lax.dot_general(
        back, weight[...], (((1,), (1,)), ((), ())), preferred_element_type=F32).astype(BF16)
    if owners == n:
        own_part()
    else:
        pl.when(me < owners)(own_part)
    for copy in pending + cot_copies + log_copies + z_copies:
        copy.wait_send()

    def drain_sib(m, carry):
        sib_copy(m).wait_send()
        return carry

    lax.fori_loop(0, O * I, drain_sib, 0)

    def drain_y(i, carry):
        zz, yy = place(i)
        y_copy(zz, yy).wait_send()
        return carry

    lax.fori_loop(0, O * (I - 1), drain_y, 0)
    by_role(sent, term_send, term_recv)
    by_role(arrived, tot_send, tot_recv)
    grad_weight[...] = total[...].reshape(grad_weight.shape)
    if owners == n:
        sent(n - 1, tot_send, tot_recv)
    else:
        @pl.when(me < owners)
        def _():
            sent(n - 1, tot_send, tot_recv)


def hand_over(a, b, c, x, y, z):
    x[...] = a[...]
    y[...] = b[...]
    z[...] = c[...]


def per_device(R, C, features, weight, tiles, slot_tile_row, tile_cols, live_tiles, cotangent):
    slots, side = tiles.shape[2], tiles.shape[3]
    stretch, width = features.shape
    out_width = weight.shape[1]
    half = C // 2
    O = 4 if half % 4 == 0 else half
    I = half // O
    n = R * C
    per = stretch // side
    cells = R * per * C * per
    owners = min(n, width // 8)
    rows = width // owners
    chunks = 8 if slots % 8 == 0 else 1
    dma = pltpu.SemaphoreType.DMA
    vmem = pltpu.VMEM
    blk = (out_width, stretch)
    gathers = (O - 1) + (I - 1) + 1 + (O - 1) * I + O * (I - 1)
    scratch = [
        vmem((slots, side, side), BF16),
        vmem((slots + 1, side, side), BF16),
        vmem((C, stretch, out_width), BF16),
        vmem((R, stretch, out_width), BF16),
        vmem((R,) + blk, BF16),
        vmem((width, stretch), BF16),
        vmem((1, slots), jnp.int32),
        vmem((1, cells), jnp.int32),
        pltpu.SMEM((1, slots), jnp.int32),
        pltpu.SMEM((1, cells), jnp.int32),
        vmem((half,) + blk, BF16),
        vmem((half,) + blk, BF16),
        vmem((half,) + blk, BF16),
        vmem((half,) + blk, BF16),
        vmem((max(O - 1, 1),) + blk, BF16),
        vmem((O,) + blk, BF16),
        vmem((max(R - 1, 1), stretch, out_width), F32),
        vmem((R, stretch, out_width), F32),
        vmem((owners, rows, out_width), F32),
        vmem((n, rows, out_width), F32),
        vmem((owners, rows, out_width), F32),
        dma((chunks,)), dma((2,)), dma((R,)), dma((R,)),
        dma((gathers,)), dma((C,)),
        dma((half,)), dma((half,)), dma((half,)), dma((half,)),
        dma((O,)), dma((O,)), dma((R,)), dma((R,)),
        dma((1,)), dma((1,)), dma((1,)), dma((1,)),
    ]
    v = pl.BlockSpec(memory_space=pltpu.VMEM)
    shapes = (
            jax.ShapeDtypeStruct((stretch, out_width), BF16),
            jax.ShapeDtypeStruct((stretch, width), BF16),
            jax.ShapeDtypeStruct((width, out_width), F32),
        )
    results = pl.pallas_call(
        functools.partial(kernel, (R, C, O, I)),
        out_shape=shapes,
        in_specs=[v, v, pl.BlockSpec(memory_space=pl.ANY), v, v,
                  pl.BlockSpec(memory_space=pltpu.SMEM), v],
        out_specs=(v, v, v),
        scratch_shapes=scratch,
        compiler_params=pltpu.CompilerParams(
            collective_id=0, has_side_effects=True, vmem_limit_bytes=60 * 1024 * 1024),
    )(features, weight, tiles.reshape(slots, side, side), slot_tile_row.reshape(1, slots),
      tile_cols.reshape(1, slots), live_tiles, cotangent)
    return pl.pallas_call(hand_over, out_shape=shapes, in_specs=[v, v, v],
                          out_specs=(v, v, v))(*results)


def solution(mesh):
    R, C = mesh.shape["row"], mesh.shape["col"]
    placed = (
        P(("row", "col"), None),
        P(),
        P("row", "col", None, None, None),
        P("row", "col", None),
        P("row", "col", None),
        P("row", "col"),
        P(("row", "col"), None),
    )
    return jax.shard_map(
        functools.partial(per_device, R, C),
        mesh=mesh,
        in_specs=placed,
        out_specs=(P(("row", "col"), None), P(("row", "col"), None), P()),
        check_vma=False,
    )
```

```python
import functools
import math

import jax
import jax.numpy as jnp
from jax import lax
from jax.experimental import pallas as pl
from jax.experimental.pallas import tpu as pltpu
from jax.sharding import PartitionSpec as P

MESH = pl.DeviceIdType.MESH
F32 = jnp.float32
BF16 = jnp.bfloat16


def kernel(dims, features, weight, tiles, slot_rows, slot_cols, live, cot,
           logits, grad_features, grad_weight,
           tile_buf, sums, proj, cots, cots_t, feat_t, code_v, last_v, code, last,
           sib_out, sib_in, y_out, y_in, z_out, z_in, log_out, log_in,
           term_out, term_in, total,
           tile_sem, smem_sem, cot_send, cot_recv, ag_send, ag_recv,
           sib_send, sib_recv, y_send, y_recv, z_send, z_recv,
           log_send, log_recv, term_send, term_recv, tot_send, tot_recv):
    R, C, O, I = dims
    n = R * C
    slots = tiles.shape[0]
    side = tiles.shape[1]
    stretch = features.shape[0]
    per = stretch // side
    col_tiles = C * per
    cells = R * per * col_tiles
    r, c = lax.axis_index("row"), lax.axis_index("col")
    me = r * C + c
    k = lax.rem(c, 2)
    q = c // 2
    y = lax.rem(q, I)
    z = q // I

    def col_of(zz, yy, kk):
        return (zz * I + yy) * 2 + kk

    def remote(src, dst, send, recv, dev):
        return pltpu.make_async_remote_copy(
            src_ref=src, dst_ref=dst, send_sem=send, recv_sem=recv,
            device_id=dev, device_id_type=MESH)

    chunks = tile_sem.shape[0]
    chunk = slots // chunks
    loads = [
        pltpu.make_async_copy(tiles.at[pl.ds(i * chunk, chunk)],
                              tile_buf.at[pl.ds(i * chunk, chunk)], tile_sem.at[i])
        for i in range(chunks)
    ]
    for load in loads:
        load.start()

    barrier = pltpu.get_barrier_semaphore()

    def greet(d, carry):
        t = lax.rem(me + d, n)
        pl.semaphore_signal(barrier, inc=1, device_id=(t // C, lax.rem(t, C)), device_id_type=MESH)
        return carry

    lax.fori_loop(1, n, greet, 0, unroll=n - 1 if n <= 32 else 1)
    proj[c] = jnp.dot(features[...], weight[...], preferred_element_type=F32).astype(BF16)
    lane = lax.broadcasted_iota(jnp.int32, (1, slots), 1)
    cell = jnp.where(lane < live[0, 0], slot_rows[...] * col_tiles + slot_cols[...], cells)
    eye = (lax.broadcasted_iota(jnp.int32, (slots, slots), 0)
           == lax.broadcasted_iota(jnp.int32, (slots, slots), 1))
    cell_c = jnp.sum(jnp.where(eye, cell, 0), axis=1, keepdims=True)
    sub = lax.broadcasted_iota(jnp.int32, (slots, 1), 0)
    same_before = (cell == cell_c) & (lane < sub)
    rank = jnp.sum(((cell < cell_c) | same_before).astype(jnp.int32), axis=1, keepdims=True)
    keep = jnp.max(same_before.astype(jnp.int32), axis=1, keepdims=True)
    code_v[...] = jnp.sum(jnp.where(rank == lane, sub * 2 + keep, 0), axis=0, keepdims=True)
    cell_ids = lax.broadcasted_iota(jnp.int32, (1, cells), 1)
    upto = jnp.sum((cell_c <= cell_ids).astype(jnp.int32), axis=0, keepdims=True)
    held = jnp.max((cell_c == cell_ids).astype(jnp.int32), axis=0, keepdims=True)
    last_v[...] = upto * held
    to_smem = [pltpu.make_async_copy(code_v, code, smem_sem.at[0]),
               pltpu.make_async_copy(last_v, last, smem_sem.at[1])]
    for copy in to_smem:
        copy.start()
    feat_t[...] = features[...].astype(F32).T.astype(BF16)
    cots_t[r] = cot[...].astype(F32).T.astype(BF16)
    sums[0] = jnp.zeros((side, side), BF16)
    pl.semaphore_wait(barrier, n - 1)

    pending = []

    def gather_send(block, dev):
        copy = remote(proj.at[block], proj.at[block], ag_send.at[len(pending)],
                      ag_recv.at[block], (r, dev))
        copy.start()
        pending.append(copy)

    def gather_wait(block):
        remote(proj.at[block], proj.at[block], ag_send.at[0], ag_recv.at[block],
               (r, c)).wait_recv()

    cot_copies = []
    for d in range(1, R):
        peer = lax.rem(r + d, R)
        copy = remote(cot, cots.at[r], cot_send.at[d], cot_recv.at[r], (peer, c))
        copy.start()
        cot_copies.append(copy)
    z_peers = [lax.rem(z + d, O) for d in range(1, O)]
    y_peers = [lax.rem(y + d, I) for d in range(1, I)]
    for yy in y_peers:
        gather_send(c, col_of(z, yy, k))
    for zz in z_peers:
        gather_send(c, col_of(zz, y, k))
    gather_send(c, col_of(z, y, 1 - k))

    for copy in to_smem:
        copy.wait()
    for load in loads:
        load.wait()

    def add_slot(j, acc):
        word = code[0, j]
        keep_it = lax.rem(word, 2).astype(F32)
        acc = acc * keep_it + tile_buf[word // 2].astype(F32)
        sums[j + 1] = acc.astype(BF16)
        return acc

    parts = 8
    acc = jnp.zeros((side, side), F32)
    for part in range(parts):
        acc = lax.fori_loop(part * slots // parts, (part + 1) * slots // parts, add_slot, acc,
                            unroll=4)
        for zz in z_peers[part - 2:part - 1] if part > 1 else []:
            block = col_of(zz, y, k)
            gather_wait(block)
            for yy in y_peers:
                gather_send(block, col_of(z, yy, k))
            gather_send(block, col_of(z, y, 1 - k))

    for d in range(1, R):
        peer = lax.rem(r + d, R)
        remote(cot, cots.at[peer], cot_send.at[d], cot_recv.at[peer], (peer, c)).wait_recv()
        cots_t[peer] = cots[peer].astype(F32).T.astype(BF16)

    def stretch_block(s, b):
        rows = []
        for a in range(per):
            base = (s * per + a) * col_tiles + b * per
            rows.append(jnp.concatenate([sums[last[0, base + e]] for e in range(per)], axis=1))
        return jnp.concatenate(rows, axis=0)

    def back_block(b):
        out = jnp.dot(cots_t[0], stretch_block(0, b), preferred_element_type=F32)
        for s in range(1, R):
            out = out + jnp.dot(cots_t[s], stretch_block(s, b), preferred_element_type=F32)
        return out

    def place(i):
        zz = lax.rem(z + lax.rem(i, O) + 1, O)
        yy = lax.rem(y + i // O + 1, I)
        return zz, yy

    def sib_copy(m):
        return remote(sib_out.at[m], sib_in.at[m], sib_send.at[m], sib_recv.at[m],
                      (r, col_of(z, y, 1 - k)))

    def send_sib(i, carry):
        zz, yy = place(i)
        m = zz * I + yy
        sib_out[m] = back_block(2 * m + 1 - k).astype(BF16)
        sib_copy(m).start()
        return carry

    lax.fori_loop(0, O * I, send_sib, 0)

    def y_copy(zz, yy):
        return remote(y_out.at[zz * I + yy], y_in.at[y * O + zz], y_send.at[zz * I + yy],
                      y_recv.at[y * O + zz], (r, col_of(z, yy, k)))

    def send_y(i, carry):
        zz, yy = place(i)
        m = zz * I + yy
        mine = back_block(2 * m + k)
        sib_copy(m).wait_recv()
        y_out[m] = (mine + sib_in[m].astype(F32)).astype(BF16)
        y_copy(zz, yy).start()
        return carry

    lax.fori_loop(0, O * (I - 1), send_y, 0)

    for d in range(O):
        zz = lax.rem(z + d, O)
        for yy in y_peers:
            block = col_of(zz, yy, k)
            gather_wait(block)
            gather_send(block, col_of(z, y, 1 - k))

    def summed(zz):
        m = zz * I + y
        value = back_block(2 * m + k)
        sib_copy(m).wait_recv()
        value = value + sib_in[m].astype(F32)
        for yy in y_peers:
            slot = yy * O + zz
            remote(y_out.at[0], y_in.at[slot], y_send.at[0], y_recv.at[slot],
                   (r, c)).wait_recv()
            value = value + y_in[slot].astype(F32)
        return value

    z_copies = []
    for d in range(1, O):
        zz = lax.rem(z + d, O)
        z_out[d - 1] = summed(zz).astype(BF16)
        copy = remote(z_out.at[d - 1], z_in.at[z], z_send.at[d - 1], z_recv.at[z],
                      (r, col_of(zz, y, k)))
        copy.start()
        z_copies.append(copy)
    for d in range(O):
        for e in range(I):
            gather_wait(col_of(lax.rem(z + d, O), lax.rem(y + e, I), 1 - k))
    group = 4 if C % 4 == 0 else 1

    def forward(s):
        def step(g, out):
            for b in range(group):
                out = out + jnp.dot(stretch_block(s, g * group + b), proj[g * group + b],
                                    preferred_element_type=F32)
            return out
        return lax.fori_loop(0, C // group, step, jnp.zeros((stretch, proj.shape[2]), F32))

    log_copies = []
    for d in range(1, R):
        peer = lax.rem(r + d, R)
        log_out[d - 1] = forward(peer)
        copy = remote(log_out.at[d - 1], log_in.at[r], log_send.at[d], log_recv.at[r], (peer, c))
        copy.start()
        log_copies.append(copy)
    mine_log = forward(r)

    back_t = summed(z)
    for zz in z_peers:
        remote(z_out.at[0], z_in.at[zz], z_send.at[0], z_recv.at[zz], (r, c)).wait_recv()
        back_t = back_t + z_in[zz].astype(F32)
    back = back_t.T.astype(BF16)
    term = jnp.dot(feat_t[...], back, preferred_element_type=F32)

    owners = term_out.shape[0]
    rows = term_out.shape[1]
    term_out[...] = term.reshape(term_out.shape)

    def term_copy(t):
        return remote(term_out.at[t], term_in.at[me], term_send.at[0], term_recv.at[0],
                      (t // C, lax.rem(t, C)))

    def bulk(count, send, recv):
        part = term_in.at[pl.ds(0, count)]
        return remote(part, part, send.at[0], recv.at[0], (r, c))

    def arrived(count, send, recv):
        bulk(count, send, recv).wait_recv()

    def sent(count, send, recv):
        bulk(count, send, recv).wait_send()

    def by_role(act, send, recv):
        if owners == n:
            act(n - 1, send, recv)
        else:
            pl.when(me < owners)(lambda: act(owners - 1, send, recv))
            pl.when(me >= owners)(lambda: act(owners, send, recv))

    def tot_copy(t):
        return remote(total.at[me], total.at[me], tot_send.at[0], tot_recv.at[0],
                      (t // C, lax.rem(t, C)))

    def others(count, act):
        def body(d, carry):
            t = lax.rem(me + d, n)
            if count == n:
                act(t)
            else:
                @pl.when(t < count)
                def _():
                    act(t)
            return carry
        lax.fori_loop(1, n, body, 0, unroll=n - 1 if n <= 32 else 1)

    def own_part():
        term_in[me] = term_out[me]
        arrived(n - 1, term_send, term_recv)
        total[me] = jnp.sum(term_in[...], axis=0) * (1.0 / math.sqrt(n * stretch))
        others(n, lambda t: tot_copy(t).start())

    others(owners, lambda t: term_copy(t).start())
    grad_features[...] = lax.dot_general(
        back, weight[...], (((1,), (1,)), ((), ())), preferred_element_type=F32).astype(BF16)
    for d in range(1, R):
        peer = lax.rem(r + d, R)
        remote(log_out.at[0], log_in.at[peer], log_send.at[0], log_recv.at[peer],
               (peer, c)).wait_recv()
        mine_log = mine_log + log_in[peer]
    logits[...] = mine_log.astype(BF16)
    if owners == n:
        own_part()
    else:
        pl.when(me < owners)(own_part)
    for copy in pending + cot_copies + log_copies + z_copies:
        copy.wait_send()

    def drain_sib(m, carry):
        sib_copy(m).wait_send()
        return carry

    lax.fori_loop(0, O * I, drain_sib, 0)

    def drain_y(i, carry):
        zz, yy = place(i)
        y_copy(zz, yy).wait_send()
        return carry

    lax.fori_loop(0, O * (I - 1), drain_y, 0)
    by_role(sent, term_send, term_recv)
    by_role(arrived, tot_send, tot_recv)
    grad_weight[...] = total[...].reshape(grad_weight.shape)
    if owners == n:
        sent(n - 1, tot_send, tot_recv)
    else:
        @pl.when(me < owners)
        def _():
            sent(n - 1, tot_send, tot_recv)


def hand_over(a, b, c, x, y, z):
    x[...] = a[...]
    y[...] = b[...]
    z[...] = c[...]


def per_device(R, C, features, weight, tiles, slot_tile_row, tile_cols, live_tiles, cotangent):
    slots, side = tiles.shape[2], tiles.shape[3]
    stretch, width = features.shape
    out_width = weight.shape[1]
    half = C // 2
    O = 4 if half % 4 == 0 else half
    I = half // O
    n = R * C
    per = stretch // side
    cells = R * per * C * per
    owners = min(n, width // 8)
    rows = width // owners
    chunks = 8 if slots % 8 == 0 else 1
    dma = pltpu.SemaphoreType.DMA
    vmem = pltpu.VMEM
    blk = (out_width, stretch)
    gathers = (O - 1) + (I - 1) + 1 + (O - 1) * I + O * (I - 1)
    scratch = [
        vmem((slots, side, side), BF16),
        vmem((slots + 1, side, side), BF16),
        vmem((C, stretch, out_width), BF16),
        vmem((R, stretch, out_width), BF16),
        vmem((R,) + blk, BF16),
        vmem((width, stretch), BF16),
        vmem((1, slots), jnp.int32),
        vmem((1, cells), jnp.int32),
        pltpu.SMEM((1, slots), jnp.int32),
        pltpu.SMEM((1, cells), jnp.int32),
        vmem((half,) + blk, BF16),
        vmem((half,) + blk, BF16),
        vmem((half,) + blk, BF16),
        vmem((half,) + blk, BF16),
        vmem((max(O - 1, 1),) + blk, BF16),
        vmem((O,) + blk, BF16),
        vmem((max(R - 1, 1), stretch, out_width), F32),
        vmem((R, stretch, out_width), F32),
        vmem((owners, rows, out_width), F32),
        vmem((n, rows, out_width), F32),
        vmem((owners, rows, out_width), F32),
        dma((chunks,)), dma((2,)), dma((R,)), dma((R,)),
        dma((gathers,)), dma((C,)),
        dma((half,)), dma((half,)), dma((half,)), dma((half,)),
        dma((O,)), dma((O,)), dma((R,)), dma((R,)),
        dma((1,)), dma((1,)), dma((1,)), dma((1,)),
    ]
    v = pl.BlockSpec(memory_space=pltpu.VMEM)
    shapes = (
            jax.ShapeDtypeStruct((stretch, out_width), BF16),
            jax.ShapeDtypeStruct((stretch, width), BF16),
            jax.ShapeDtypeStruct((width, out_width), F32),
        )
    results = pl.pallas_call(
        functools.partial(kernel, (R, C, O, I)),
        out_shape=shapes,
        in_specs=[v, v, pl.BlockSpec(memory_space=pl.ANY), v, v,
                  pl.BlockSpec(memory_space=pltpu.SMEM), v],
        out_specs=(v, v, v),
        scratch_shapes=scratch,
        compiler_params=pltpu.CompilerParams(
            collective_id=0, has_side_effects=True, vmem_limit_bytes=60 * 1024 * 1024),
    )(features, weight, tiles.reshape(slots, side, side), slot_tile_row.reshape(1, slots),
      tile_cols.reshape(1, slots), live_tiles, cotangent)
    return pl.pallas_call(hand_over, out_shape=shapes, in_specs=[v, v, v],
                          out_specs=(v, v, v))(*results)


def solution(mesh):
    R, C = mesh.shape["row"], mesh.shape["col"]
    placed = (
        P(("row", "col"), None),
        P(),
        P("row", "col", None, None, None),
        P("row", "col", None),
        P("row", "col", None),
        P("row", "col"),
        P(("row", "col"), None),
    )
    return jax.shard_map(
        functools.partial(per_device, R, C),
        mesh=mesh,
        in_specs=placed,
        out_specs=(P(("row", "col"), None), P(("row", "col"), None), P()),
        check_vma=False,
    )
```

```python
import functools
import math

import jax
import jax.numpy as jnp
from jax import lax
from jax.experimental import pallas as pl
from jax.experimental.pallas import tpu as pltpu
from jax.sharding import PartitionSpec as P

MESH = pl.DeviceIdType.MESH
F32 = jnp.float32
BF16 = jnp.bfloat16


def kernel(dims, features, weight, tiles, slot_rows, slot_cols, live, cot,
           logits, grad_features, grad_weight,
           tile_buf, sums, proj, cots, cots_t, feat_t, code_v, last_v, code, last,
           sib_out, sib_in, y_out, y_in, z_out, z_in, log_out, log_in,
           term_out, term_in, total,
           tile_sem, smem_sem, cot_send, cot_recv, ag_send, ag_recv,
           sib_send, sib_recv, y_send, y_recv, z_send, z_recv,
           log_send, log_recv, term_send, term_recv, tot_send, tot_recv):
    R, C, O, I = dims
    n = R * C
    slots = tiles.shape[0]
    side = tiles.shape[1]
    stretch = features.shape[0]
    per = stretch // side
    col_tiles = C * per
    cells = R * per * col_tiles
    r, c = lax.axis_index("row"), lax.axis_index("col")
    me = r * C + c
    k = lax.rem(c, 2)
    q = c // 2
    y = lax.rem(q, I)
    z = q // I

    def col_of(zz, yy, kk):
        return (zz * I + yy) * 2 + kk

    def remote(src, dst, send, recv, dev):
        return pltpu.make_async_remote_copy(
            src_ref=src, dst_ref=dst, send_sem=send, recv_sem=recv,
            device_id=dev, device_id_type=MESH)

    chunks = tile_sem.shape[0]
    chunk = slots // chunks
    loads = [
        pltpu.make_async_copy(tiles.at[pl.ds(i * chunk, chunk)],
                              tile_buf.at[pl.ds(i * chunk, chunk)], tile_sem.at[i])
        for i in range(chunks)
    ]
    for load in loads:
        load.start()

    barrier = pltpu.get_barrier_semaphore()

    def greet(d, carry):
        t = lax.rem(me + d, n)
        pl.semaphore_signal(barrier, inc=1, device_id=(t // C, lax.rem(t, C)), device_id_type=MESH)
        return carry

    lax.fori_loop(1, n, greet, 0, unroll=n - 1 if n <= 32 else 1)
    proj[c] = jnp.dot(features[...], weight[...], preferred_element_type=F32).astype(BF16)
    lane = lax.broadcasted_iota(jnp.int32, (1, slots), 1)
    cell = jnp.where(lane < live[0, 0], slot_rows[...] * col_tiles + slot_cols[...], cells)
    eye = (lax.broadcasted_iota(jnp.int32, (slots, slots), 0)
           == lax.broadcasted_iota(jnp.int32, (slots, slots), 1))
    cell_c = jnp.sum(jnp.where(eye, cell, 0), axis=1, keepdims=True)
    sub = lax.broadcasted_iota(jnp.int32, (slots, 1), 0)
    same_before = (cell == cell_c) & (lane < sub)
    rank = jnp.sum(((cell < cell_c) | same_before).astype(jnp.int32), axis=1, keepdims=True)
    keep = jnp.max(same_before.astype(jnp.int32), axis=1, keepdims=True)
    code_v[...] = jnp.sum(jnp.where(rank == lane, sub * 2 + keep, 0), axis=0, keepdims=True)
    cell_ids = lax.broadcasted_iota(jnp.int32, (1, cells), 1)
    upto = jnp.sum((cell_c <= cell_ids).astype(jnp.int32), axis=0, keepdims=True)
    held = jnp.max((cell_c == cell_ids).astype(jnp.int32), axis=0, keepdims=True)
    last_v[...] = upto * held
    to_smem = [pltpu.make_async_copy(code_v, code, smem_sem.at[0]),
               pltpu.make_async_copy(last_v, last, smem_sem.at[1])]
    for copy in to_smem:
        copy.start()
    feat_t[...] = features[...].astype(F32).T.astype(BF16)
    cots_t[r] = cot[...].astype(F32).T.astype(BF16)
    sums[0] = jnp.zeros((side, side), BF16)
    pl.semaphore_wait(barrier, n - 1)

    pending = []

    def gather_send(block, dev):
        copy = remote(proj.at[block], proj.at[block], ag_send.at[len(pending)],
                      ag_recv.at[block], (r, dev))
        copy.start()
        pending.append(copy)

    def gather_wait(block):
        remote(proj.at[block], proj.at[block], ag_send.at[0], ag_recv.at[block],
               (r, c)).wait_recv()

    cot_copies = []
    for d in range(1, R):
        peer = lax.rem(r + d, R)
        copy = remote(cot, cots.at[r], cot_send.at[d], cot_recv.at[r], (peer, c))
        copy.start()
        cot_copies.append(copy)
    z_peers = [lax.rem(z + d, O) for d in range(1, O)]
    y_peers = [lax.rem(y + d, I) for d in range(1, I)]
    for yy in y_peers:
        gather_send(c, col_of(z, yy, k))
    for zz in z_peers:
        gather_send(c, col_of(zz, y, k))
    gather_send(c, col_of(z, y, 1 - k))

    for copy in to_smem:
        copy.wait()
    for load in loads:
        load.wait()

    def add_slot(j, acc):
        word = code[0, j]
        keep_it = lax.rem(word, 2).astype(F32)
        acc = acc * keep_it + tile_buf[word // 2].astype(F32)
        sums[j + 1] = acc.astype(BF16)
        return acc

    parts = 8
    acc = jnp.zeros((side, side), F32)
    for part in range(parts):
        acc = lax.fori_loop(part * slots // parts, (part + 1) * slots // parts, add_slot, acc,
                            unroll=4)
        for zz in z_peers[part - 2:part - 1] if part > 1 else []:
            block = col_of(zz, y, k)
            gather_wait(block)
            for yy in y_peers:
                gather_send(block, col_of(z, yy, k))
            gather_send(block, col_of(z, y, 1 - k))

    for d in range(1, R):
        peer = lax.rem(r + d, R)
        remote(cot, cots.at[peer], cot_send.at[d], cot_recv.at[peer], (peer, c)).wait_recv()
        cots_t[peer] = cots[peer].astype(F32).T.astype(BF16)

    def stretch_block(s, b):
        rows = []
        for a in range(per):
            base = (s * per + a) * col_tiles + b * per
            rows.append(jnp.concatenate([sums[last[0, base + e]] for e in range(per)], axis=1))
        return jnp.concatenate(rows, axis=0)

    def back_block(b):
        out = jnp.dot(cots_t[0], stretch_block(0, b), preferred_element_type=F32)
        for s in range(1, R):
            out = out + jnp.dot(cots_t[s], stretch_block(s, b), preferred_element_type=F32)
        return out

    def place(i):
        zz = lax.rem(z + lax.rem(i, O) + 1, O)
        yy = lax.rem(y + i // O + 1, I)
        return zz, yy

    def sib_copy(m):
        return remote(sib_out.at[m], sib_in.at[m], sib_send.at[m], sib_recv.at[m],
                      (r, col_of(z, y, 1 - k)))

    def send_sib(i, carry):
        zz, yy = place(i)
        m = zz * I + yy
        sib_out[m] = back_block(2 * m + 1 - k).astype(BF16)
        sib_copy(m).start()
        return carry

    lax.fori_loop(0, O * I, send_sib, 0)

    def y_copy(zz, yy):
        return remote(y_out.at[zz * I + yy], y_in.at[y * O + zz], y_send.at[zz * I + yy],
                      y_recv.at[y * O + zz], (r, col_of(z, yy, k)))

    def send_y(i, carry):
        zz, yy = place(i)
        m = zz * I + yy
        mine = back_block(2 * m + k)
        sib_copy(m).wait_recv()
        y_out[m] = (mine + sib_in[m].astype(F32)).astype(BF16)
        y_copy(zz, yy).start()
        return carry

    lax.fori_loop(0, O * (I - 1), send_y, 0)

    for d in range(O):
        zz = lax.rem(z + d, O)
        for yy in y_peers:
            block = col_of(zz, yy, k)
            gather_wait(block)
            gather_send(block, col_of(z, y, 1 - k))

    def summed(zz):
        m = zz * I + y
        value = back_block(2 * m + k)
        sib_copy(m).wait_recv()
        value = value + sib_in[m].astype(F32)
        for yy in y_peers:
            slot = yy * O + zz
            remote(y_out.at[0], y_in.at[slot], y_send.at[0], y_recv.at[slot],
                   (r, c)).wait_recv()
            value = value + y_in[slot].astype(F32)
        return value

    z_copies = []
    for d in range(1, O):
        zz = lax.rem(z + d, O)
        z_out[d - 1] = summed(zz).astype(BF16)
        copy = remote(z_out.at[d - 1], z_in.at[z], z_send.at[d - 1], z_recv.at[z],
                      (r, col_of(zz, y, k)))
        copy.start()
        z_copies.append(copy)
    for d in range(O):
        for e in range(I):
            gather_wait(col_of(lax.rem(z + d, O), lax.rem(y + e, I), 1 - k))
    group = 4 if C % 4 == 0 else 1

    def forward(s):
        def step(g, out):
            for b in range(group):
                out = out + jnp.dot(stretch_block(s, g * group + b), proj[g * group + b],
                                    preferred_element_type=F32)
            return out
        return lax.fori_loop(0, C // group, step, jnp.zeros((stretch, proj.shape[2]), F32))

    log_copies = []
    for d in range(1, R):
        peer = lax.rem(r + d, R)
        log_out[d - 1] = forward(peer)
        copy = remote(log_out.at[d - 1], log_in.at[r], log_send.at[d], log_recv.at[r], (peer, c))
        copy.start()
        log_copies.append(copy)
    mine_log = forward(r)

    back_t = summed(z)
    for zz in z_peers:
        remote(z_out.at[0], z_in.at[zz], z_send.at[0], z_recv.at[zz], (r, c)).wait_recv()
        back_t = back_t + z_in[zz].astype(F32)
    back = back_t.T.astype(BF16)
    term = jnp.dot(feat_t[...], back, preferred_element_type=F32)

    owners = term_out.shape[0]
    rows = term_out.shape[1]
    term_out[...] = term.reshape(term_out.shape).astype(BF16)

    def term_copy(t):
        return remote(term_out.at[t], term_in.at[me], term_send.at[0], term_recv.at[0],
                      (t // C, lax.rem(t, C)))

    def bulk(count, send, recv):
        part = (term_in if send is term_send else total).at[pl.ds(0, count)]
        return remote(part, part, send.at[0], recv.at[0], (r, c))

    def arrived(count, send, recv):
        bulk(count, send, recv).wait_recv()

    def sent(count, send, recv):
        bulk(count, send, recv).wait_send()

    def by_role(act, send, recv):
        if owners == n:
            act(n - 1, send, recv)
        else:
            pl.when(me < owners)(lambda: act(owners - 1, send, recv))
            pl.when(me >= owners)(lambda: act(owners, send, recv))

    def tot_copy(t):
        return remote(total.at[me], total.at[me], tot_send.at[0], tot_recv.at[0],
                      (t // C, lax.rem(t, C)))

    def others(count, act):
        def body(d, carry):
            t = lax.rem(me + d, n)
            if count == n:
                act(t)
            else:
                @pl.when(t < count)
                def _():
                    act(t)
            return carry
        lax.fori_loop(1, n, body, 0, unroll=n - 1 if n <= 32 else 1)

    def own_part():
        term_in[me] = term_out[me]
        arrived(n - 1, term_send, term_recv)
        total[me] = jnp.sum(term_in[...].astype(F32), axis=0) * (1.0 / math.sqrt(n * stretch))
        others(n, lambda t: tot_copy(t).start())

    others(owners, lambda t: term_copy(t).start())
    grad_features[...] = lax.dot_general(
        back, weight[...], (((1,), (1,)), ((), ())), preferred_element_type=F32).astype(BF16)
    for d in range(1, R):
        peer = lax.rem(r + d, R)
        remote(log_out.at[0], log_in.at[peer], log_send.at[0], log_recv.at[peer],
               (peer, c)).wait_recv()
        mine_log = mine_log + log_in[peer]
    logits[...] = mine_log.astype(BF16)
    if owners == n:
        own_part()
    else:
        pl.when(me < owners)(own_part)
    for copy in pending + cot_copies + log_copies + z_copies:
        copy.wait_send()

    def drain_sib(m, carry):
        sib_copy(m).wait_send()
        return carry

    lax.fori_loop(0, O * I, drain_sib, 0)

    def drain_y(i, carry):
        zz, yy = place(i)
        y_copy(zz, yy).wait_send()
        return carry

    lax.fori_loop(0, O * (I - 1), drain_y, 0)
    by_role(sent, term_send, term_recv)
    by_role(arrived, tot_send, tot_recv)
    grad_weight[...] = total[pl.ds(0, owners)].reshape(grad_weight.shape)
    if owners == n:
        sent(n - 1, tot_send, tot_recv)
    else:
        @pl.when(me < owners)
        def _():
            sent(n - 1, tot_send, tot_recv)


def hand_over(a, b, c, x, y, z):
    x[...] = a[...]
    y[...] = b[...]
    z[...] = c[...]


def per_device(R, C, features, weight, tiles, slot_tile_row, tile_cols, live_tiles, cotangent):
    slots, side = tiles.shape[2], tiles.shape[3]
    stretch, width = features.shape
    out_width = weight.shape[1]
    half = C // 2
    O = 4 if half % 4 == 0 else half
    I = half // O
    n = R * C
    per = stretch // side
    cells = R * per * C * per
    owners = min(n, width // 8)
    rows = width // owners
    chunks = 8 if slots % 8 == 0 else 1
    dma = pltpu.SemaphoreType.DMA
    vmem = pltpu.VMEM
    blk = (out_width, stretch)
    gathers = (O - 1) + (I - 1) + 1 + (O - 1) * I + O * (I - 1)
    scratch = [
        vmem((slots, side, side), BF16),
        vmem((slots + 1, side, side), BF16),
        vmem((C, stretch, out_width), BF16),
        vmem((R, stretch, out_width), BF16),
        vmem((R,) + blk, BF16),
        vmem((width, stretch), BF16),
        vmem((1, slots), jnp.int32),
        vmem((1, cells), jnp.int32),
        pltpu.SMEM((1, slots), jnp.int32),
        pltpu.SMEM((1, cells), jnp.int32),
        vmem((half,) + blk, BF16),
        vmem((half,) + blk, BF16),
        vmem((half,) + blk, BF16),
        vmem((half,) + blk, BF16),
        vmem((max(O - 1, 1),) + blk, BF16),
        vmem((O,) + blk, BF16),
        vmem((max(R - 1, 1), stretch, out_width), F32),
        vmem((R, stretch, out_width), F32),
        vmem((owners, rows, out_width), BF16),
        vmem((n, rows, out_width), BF16),
        vmem((n, rows, out_width), F32),
        dma((chunks,)), dma((2,)), dma((R,)), dma((R,)),
        dma((gathers,)), dma((C,)),
        dma((half,)), dma((half,)), dma((half,)), dma((half,)),
        dma((O,)), dma((O,)), dma((R,)), dma((R,)),
        dma((1,)), dma((1,)), dma((1,)), dma((1,)),
    ]
    v = pl.BlockSpec(memory_space=pltpu.VMEM)
    shapes = (
            jax.ShapeDtypeStruct((stretch, out_width), BF16),
            jax.ShapeDtypeStruct((stretch, width), BF16),
            jax.ShapeDtypeStruct((width, out_width), F32),
        )
    results = pl.pallas_call(
        functools.partial(kernel, (R, C, O, I)),
        out_shape=shapes,
        in_specs=[v, v, pl.BlockSpec(memory_space=pl.ANY), v, v,
                  pl.BlockSpec(memory_space=pltpu.SMEM), v],
        out_specs=(v, v, v),
        scratch_shapes=scratch,
        compiler_params=pltpu.CompilerParams(
            collective_id=0, has_side_effects=True, vmem_limit_bytes=60 * 1024 * 1024),
    )(features, weight, tiles.reshape(slots, side, side), slot_tile_row.reshape(1, slots),
      tile_cols.reshape(1, slots), live_tiles, cotangent)
    return pl.pallas_call(hand_over, out_shape=shapes, in_specs=[v, v, v],
                          out_specs=(v, v, v))(*results)


def solution(mesh):
    R, C = mesh.shape["row"], mesh.shape["col"]
    placed = (
        P(("row", "col"), None),
        P(),
        P("row", "col", None, None, None),
        P("row", "col", None),
        P("row", "col", None),
        P("row", "col"),
        P(("row", "col"), None),
    )
    return jax.shard_map(
        functools.partial(per_device, R, C),
        mesh=mesh,
        in_specs=placed,
        out_specs=(P(("row", "col"), None), P(("row", "col"), None), P()),
        check_vma=False,
    )
```
